32 devices in a mesh: gx: 4 (over y, core), gy: 8 (over z, x).
Axes of the slice: x: 2, y: 2, z: 4, core: 2. Of those that a mesh axis runs over, the one named last changes fastest.
Arguments:
- basis: float32 [3, 400, 4, 10240], P(None, None, 'gx', 'gy'), may hold values from -0.3125 to 0.3125
- connectivity: int32 [8, 4, 8192], P(None, 'gx', 'gy'), may hold values from 0 to 1791
- send_nodes: int32 [4, 4, 1024], P(None, 'gx', 'gy'), may hold values from 0 to 1279
- modulus: float32 [4, 8192], P('gx', 'gy'), may hold values from 0.2 to 5
- ecsw_weight: float32 [4, 8192], P('gx', 'gy'), may hold values from 0.3 to 6
- stiffness: float32 [24, 24], replicated, may hold values from -1.25 to 1.25
- coords: float32 [400], replicated, may hold values from -6 to 6
- velocity: float32 [400], replicated, may hold values from -3 to 3
- external: float32 [400], replicated, may hold values from -12 to 12
Outputs:
- final_coords: float32 [400], replicated
- final_velocity: float32 [400], replicated
- reduced_force: float32 [400], replicated
- displaced: float32 [3, 4, 10240], P(None, 'gx', 'gy')
The draws below stay inside these ranges and needn't reach their ends.
Inputs may be any that keep to these rules, and one draw needn't show every extreme that they name: `connectivity`: entries index a partition's node table: its 1280 owned nodes, then 128 nodes from each of the neighbours below and above along gx, then below and above along gy. `send_nodes`: Owned-node indices of a partition, 128 for each neighbour, in the order below and above along gx, below and above along gy; an index may repeat.
All inputs are finite; a program needn't handle non-finite values.
Results may differ from the reference program's by a relative error of at most 0.0003.
Values sent between devices are 32-bit elements; how exact they have to be, the bound alone decides.
A program may use at most 128 MiB of HBM per device.

```python
import math
import jax
import jax.numpy as jnp
from jax import lax

K = 400
NODES_DEV = 1280
ELEM_DEV = 1024
HALO = 128
STEPS = 2
SLOTS = 1792
ELEMENTS = 8192
NODES = 10240
N_GX = 4
N_GY = 8


def set_ends(drawn, rng, least, largest):
    longest = drawn.shape.index(max(drawn.shape))
    spots = []
    for shift in (0, 1):
        where = [jax.random.randint(jax.random.fold_in(rng, axis), (), 0, length) for axis, length in enumerate(drawn.shape)]
        where[longest] = (where[longest] + shift) % drawn.shape[longest]
        spots.append(tuple(where))
    return drawn.at[spots[0]].set(least).at[spots[1]].set(largest)


def block_levels(stream_key, shape, shards, least, high):
    loudness = 1.0
    for position, blocks in shards:
        heights = jax.random.uniform(jax.random.fold_in(jax.random.fold_in(stream_key, 6), position), (blocks,), jnp.float32, least / len(shards), high / len(shards))
        loudness = loudness * jnp.repeat(jnp.exp(heights), shape[position] // blocks).reshape((-1,) + (1,) * (len(shape) - 1 - position))
    return loudness


def gaussian(own_key, shape, scale, most, split=(), dtype=jnp.bfloat16):
    drawn = scale * jax.random.normal(own_key, shape, jnp.float32)
    if split:
        drawn = drawn * block_levels(own_key, shape, split, -0.22, 0.18)
    return jnp.clip(drawn, -most, most).astype(dtype)


def setup_inputs(seed: int = 0) -> dict:
    keys = jax.random.split(jax.random.key(seed), 10)
    return {
        "basis": gaussian(keys[0], (3, K, N_GX, NODES), K ** -0.5, 0.3125, ((2, 4), (3, 8)), jnp.float32),
        "connectivity": set_ends(jax.random.randint(keys[1], (8, N_GX, ELEMENTS), 0, SLOTS), jax.random.fold_in(keys[1], 1), 0, SLOTS - 1).astype(jnp.int32),
        "send_nodes": set_ends(jax.random.randint(keys[2], (4, N_GX, N_GY * HALO), 0, NODES_DEV), jax.random.fold_in(keys[2], 1), 0, NODES_DEV - 1).astype(jnp.int32),
        "modulus": jnp.clip(jnp.exp(math.log(5.0) - 3.218876 * jax.random.uniform(keys[3], (N_GX, ELEMENTS), jnp.float32) ** block_levels(keys[3], (N_GX, ELEMENTS), ((0, 4), (1, 8)), -0.2, 0.2)), 0.2, 5.0),
        "ecsw_weight": jnp.clip(jnp.exp(math.log(6.0) - 2.9957322 * jax.random.uniform(keys[4], (N_GX, ELEMENTS), jnp.float32) ** block_levels(keys[4], (N_GX, ELEMENTS), ((0, 4), (1, 8)), -0.2, 0.2)), 0.3, 6.0),
        "stiffness": gaussian(keys[5], (24, 24), 24 ** -0.5, 1.25, (), jnp.float32),
        "coords": gaussian(keys[6], (K,), 1.0, 6.0, (), jnp.float32),
        "velocity": gaussian(keys[7], (K,), 0.5, 3.0, (), jnp.float32),
        "external": gaussian(keys[8], (K,), 2.0, 12.0, (), jnp.float32),
    }


time_step = 0.05


def lower(array, axis):
    widths = [(0, 0)] * array.ndim
    widths[axis] = (1, 0)
    return lax.slice_in_dim(jnp.pad(array, widths), 0, array.shape[axis], axis=axis)


def upper(array, axis):
    widths = [(0, 0)] * array.ndim
    widths[axis] = (0, 1)
    return lax.slice_in_dim(jnp.pad(array, widths), 1, array.shape[axis] + 1, axis=axis)


def element_forces(moved, links, stiffness, factor):
    corner = moved[:, links]
    stacked = corner.reshape(24, links.shape[1])
    strain = jnp.dot(stiffness, stacked, precision=lax.Precision.HIGHEST)
    forces = factor * (strain + strain * strain * strain / 3.0)
    return jnp.zeros_like(moved).at[:, links].add(forces.reshape(3, 8, links.shape[1]))


def add_back(owned, indices, values):
    return owned.at[:, indices].add(values)


def reference(basis, connectivity, send_nodes, modulus, ecsw_weight, stiffness, coords, velocity, external):
    parts = N_GX * N_GY
    phi = basis.reshape(3, K, N_GX, N_GY, NODES_DEV)
    links = connectivity.reshape(8, parts, ELEM_DEV)
    senders = send_nodes.reshape(4, N_GX, N_GY, HALO)
    factor = (modulus * ecsw_weight).reshape(parts, ELEM_DEV)
    reduced = jnp.zeros_like(coords)
    for repeat in range(STEPS):
        moved = jnp.einsum("ckxyn,k->cxyn", phi, coords, precision=lax.Precision.HIGHEST)
        blocks = [jnp.take_along_axis(moved, jnp.broadcast_to(senders[side][None], (3, N_GX, N_GY, HALO)), axis=3) for side in range(4)]
        slots = [lower(blocks[1], 1), upper(blocks[0], 1), lower(blocks[3], 2), upper(blocks[2], 2)]
        lookup = jnp.concatenate([moved] + slots, axis=3).reshape(3, parts, SLOTS)
        nodal = jax.vmap(element_forces, in_axes=(1, 1, None, 0), out_axes=1)(lookup, links, stiffness, factor)
        nodal = nodal.reshape(3, N_GX, N_GY, SLOTS)
        margin = [nodal[..., NODES_DEV + side * HALO:NODES_DEV + (side + 1) * HALO] for side in range(4)]
        back = [lower(margin[1], 1), upper(margin[0], 1), lower(margin[3], 2), upper(margin[2], 2)]
        owned = nodal[..., :NODES_DEV].reshape(3, parts, NODES_DEV)
        for side in range(4):
            owned = jax.vmap(add_back, in_axes=(1, 0, 1), out_axes=1)(owned, senders[side].reshape(parts, HALO), back[side].reshape(3, parts, HALO))
        owned = owned.reshape(3, N_GX, N_GY, NODES_DEV)
        reduced = jnp.einsum("ckxyn,cxyn->k", phi, owned, precision=lax.Precision.HIGHEST)
        velocity = velocity + time_step * (external - reduced)
        coords = coords + time_step * velocity
    displaced = jnp.einsum("ckxyn,k->cxyn", phi, coords, precision=lax.Precision.HIGHEST)
    return coords, velocity, reduced, displaced.reshape(3, N_GX, N_GY * NODES_DEV)
```

```python
import functools

import jax
import jax.numpy as jnp
from jax import lax
from jax.experimental import pallas as pl
from jax.experimental.pallas import tpu as pltpu
from jax.sharding import PartitionSpec as P

STEPS = 2
LANES = 128
SUB = 8

time_step = 0.05

MESH = pl.DeviceIdType.MESH


def split(x):
    high = x.astype(jnp.bfloat16).astype(jnp.float32)
    return high, x - high


def kernel(
    sizes,
    basis_hbm,
    links_ref,
    senders_ref,
    modulus_ref,
    weight_ref,
    stiffness_ref,
    coords_ref,
    velocity_ref,
    external_ref,
    coords_out,
    velocity_out,
    reduced_out,
    displaced_out,
    raw,
    phi,
    column,
    vectors,
    table,
    factor,
    forces,
    left_hand,
    right_hand,
    left_back,
    right_back,
    own_force,
    send_u,
    recv_u,
    send_f,
    recv_f,
    sum_x,
    sum_y,
    load_sem,
    u_send_sem,
    u_recv_sem,
    f_send_sem,
    f_recv_sem,
    x_send_sem,
    x_recv_sem,
    y_send_sem,
    y_recv_sem,
):
    modes, tiles, corners, chunks, n_x, n_y = sizes
    blocks = pl.cdiv(modes, LANES)
    table_rows = table.shape[1]
    ix = lax.axis_index("gx")
    iy = lax.axis_index("gy")

    loads = [
        pltpu.make_async_copy(
            basis_hbm.at[pl.ds(c * modes * tiles, modes * tiles), :], raw.at[c], load_sem.at[c]
        )
        for c in range(3)
    ]
    for load in loads:
        load.start()

    recv_u[...] = jnp.zeros_like(recv_u)
    recv_f[...] = jnp.zeros_like(recv_f)
    send_u[...] = jnp.zeros_like(send_u)
    send_f[...] = jnp.zeros_like(send_f)
    sum_x[...] = jnp.zeros_like(sum_x)
    sum_y[...] = jnp.zeros_like(sum_y)

    barrier = pltpu.get_barrier_semaphore()
    for d in range(1, n_x):
        pl.semaphore_signal(
            barrier, inc=1, device_id={"gx": lax.rem(ix + d, n_x)}, device_id_type=MESH
        )
    for d in range(1, n_y):
        pl.semaphore_signal(
            barrier, inc=1, device_id={"gy": lax.rem(iy + d, n_y)}, device_id_type=MESH
        )

    neighbours = [
        (ix > 0, {"gx": lax.rem(ix + n_x - 1, n_x)}),
        (ix < n_x - 1, {"gx": lax.rem(ix + 1, n_x)}),
        (iy > 0, {"gy": lax.rem(iy + n_y - 1, n_y)}),
        (iy < n_y - 1, {"gy": lax.rem(iy + 1, n_y)}),
    ]

    vectors[...] = jnp.zeros_like(vectors)
    for place, ref in enumerate((coords_ref, velocity_ref, external_ref)):
        for j in range(blocks):
            width = min(LANES, modes - j * LANES)
            vectors[place, j : j + 1, :width] = ref[:, j * LANES : j * LANES + width]

    lane = lax.broadcasted_iota(jnp.int32, (LANES, LANES), 1)
    sublane = lax.broadcasted_iota(jnp.int32, (LANES, LANES), 0)
    eye = lane == sublane

    def spread_coords():
        for j in range(blocks):
            height = min(LANES, modes - j * LANES)
            row = jnp.broadcast_to(vectors[0, j : j + 1, :], (height, LANES))
            picked = jnp.where(eye[:height], row, 0.0)
            column[j * LANES : j * LANES + height, :] = jnp.broadcast_to(
                jnp.sum(picked, axis=1, keepdims=True), (height, LANES)
            )

    def fold(product):
        parts = [product[SUB * i : SUB * (i + 1)] for i in range(modes // SUB)]
        while len(parts) > 1:
            nxt = [parts[i] + parts[i + 1] for i in range(0, len(parts) - 1, 2)]
            if len(parts) % 2:
                nxt.append(parts[-1])
            parts = nxt
        return jnp.sum(parts[0], axis=0, keepdims=True)

    def move_tile(t, c):
        rows = raw[c, pl.ds(t, modes, stride=tiles), :]
        phi[c, t] = rows
        table[c, pl.ds(t, 1), :] = fold(rows * column[:modes, :])

    def displace(t):
        spread = column[:modes, :]
        for c in range(3):
            table[c, pl.ds(t, 1), :] = fold(phi[c, t] * spread)

    low_rows = sublane
    factor[...] = modulus_ref[...] * weight_ref[...]
    for chunk in range(corners * chunks):
        low = jnp.broadcast_to(links_ref[chunk : chunk + 1, :] & (LANES - 1), (LANES, LANES))
        right_hand[:, chunk * LANES : (chunk + 1) * LANES] = jnp.where(
            low == low_rows, 1.0, 0.0
        ).astype(jnp.bfloat16)
    for side in range(4):
        low = jnp.broadcast_to(senders_ref[side : side + 1, :] & (LANES - 1), (LANES, LANES))
        right_back[:, side * LANES : (side + 1) * LANES] = jnp.where(
            low == low_rows, 1.0, 0.0
        ).astype(jnp.bfloat16)
    table[...] = jnp.zeros_like(table)
    spread_coords()

    for c in range(3):
        loads[c].wait()
        pl.loop(0, tiles)(functools.partial(move_tile, c=c))

    pl.semaphore_wait(barrier, n_x + n_y - 2)

    high_rows = lax.broadcasted_iota(jnp.int32, (table_rows, LANES), 0)
    contract = (((1,), (1,)), ((), ()))

    def exchange(step, source, target, send_sem, recv_sem):
        copies = []
        for side, (exists, where) in enumerate(neighbours):
            copies.append(
                pltpu.make_async_remote_copy(
                    src_ref=source.at[step, side],
                    dst_ref=target.at[step, side ^ 1],
                    send_sem=send_sem.at[step, side],
                    recv_sem=recv_sem.at[step, side ^ 1],
                    device_id=where,
                    device_id_type=MESH,
                )
            )
        for side, (exists, where) in enumerate(neighbours):
            pl.when(exists)(copies[side].start)
        for side, (exists, where) in enumerate(neighbours):
            arrived = pltpu.make_async_remote_copy(
                src_ref=source.at[step, side],
                dst_ref=target.at[step, side],
                send_sem=send_sem.at[step, side],
                recv_sem=recv_sem.at[step, side],
                device_id=where,
                device_id_type=MESH,
            )
            pl.when(exists)(arrived.wait_recv)
        return lambda: [
            pl.when(exists)(copies[side].wait_send)
            for side, (exists, where) in enumerate(neighbours)
        ]

    def total(step, slots, axis, me, size, send_sem, recv_sem):
        copies = []
        for d in range(1, size):
            copies.append(
                pltpu.make_async_remote_copy(
                    src_ref=slots.at[step, me],
                    dst_ref=slots.at[step, me],
                    send_sem=send_sem.at[step, d],
                    recv_sem=recv_sem.at[step, me],
                    device_id={axis: lax.rem(me + d, size)},
                    device_id_type=MESH,
                )
            )
            copies[-1].start()
        for d in range(1, size):
            other = lax.rem(me + d, size)
            pltpu.make_async_remote_copy(
                src_ref=slots.at[step, other],
                dst_ref=slots.at[step, other],
                send_sem=send_sem.at[step, d],
                recv_sem=recv_sem.at[step, other],
                device_id={axis: other},
                device_id_type=MESH,
            ).wait_recv()
        value = slots[step, 0]
        for i in range(1, size):
            value = value + slots[step, i]
        return value, lambda: [copy.wait_send() for copy in copies]

    def gather(index, rows):
        low = index & (LANES - 1)
        high = lax.shift_right_logical(index, 7)
        found = [jnp.zeros(index.shape, jnp.float32) for _ in range(3)]
        for r in range(rows):
            here = high == r
            for c in range(3):
                row = jnp.broadcast_to(table[c, r : r + 1, :], index.shape)
                taken = jnp.take_along_axis(row, low, axis=1, mode="promise_in_bounds")
                found[c] = jnp.where(here, taken, found[c])
        return found

    senders = jnp.concatenate([senders_ref[...], jnp.zeros((4, LANES), jnp.int32)], axis=0)

    def place(target, chunk, index, values):
        here = jnp.broadcast_to(lax.shift_right_logical(index, 7), high_rows.shape) == high_rows
        for i, value in enumerate(values):
            target[i * table_rows : (i + 1) * table_rows, chunk * LANES : (chunk + 1) * LANES] = (
                jnp.where(here, jnp.broadcast_to(value, high_rows.shape), 0.0).astype(jnp.bfloat16)
            )

    def advance(step):
        for c, found in enumerate(gather(senders, tiles)):
            for side in range(4):
                send_u[step, side, c : c + 1, :] = found[side : side + 1, :]
        sent_u = exchange(step, send_u, recv_u, u_send_sem, u_recv_sem)
        for side in range(4):
            for c in range(3):
                table[c, tiles + side : tiles + side + 1, :] = recv_u[step, side, c : c + 1, :]

        moved = [None] * (3 * corners)
        for q in range(corners):
            index = links_ref[q * chunks : (q + 1) * chunks, :]
            for c, found in enumerate(gather(index, tiles + 4)):
                moved[c * corners + q] = found
        for i in range(3 * corners):
            strain = stiffness_ref[i, 0] * moved[0]
            for j in range(1, 3 * corners):
                strain = strain + stiffness_ref[i, j] * moved[j]
            force = factor[...] * (strain + strain * strain * strain * (1.0 / 3.0))
            high, low = split(force)
            forces[0, i] = high
            forces[1, i] = low
        for q in range(corners):
            for s in range(chunks):
                chunk = q * chunks + s
                place(
                    left_hand,
                    chunk,
                    links_ref[chunk : chunk + 1, :],
                    [
                        forces[h, c * corners + q, s : s + 1, :]
                        for c in range(3)
                        for h in range(2)
                    ],
                )
        nodal = lax.dot_general(
            left_hand[...], right_hand[...], contract, preferred_element_type=jnp.float32
        )
        for c in range(3):
            base = 2 * c * table_rows
            both = nodal[base : base + table_rows] + nodal[base + table_rows : base + 2 * table_rows]
            own_force[c] = both
            for side in range(4):
                send_f[step, side, c : c + 1, :] = both[tiles + side : tiles + side + 1]
        sent_f = exchange(step, send_f, recv_f, f_send_sem, f_recv_sem)
        for side in range(4):
            values = []
            for c in range(3):
                values.extend(split(recv_f[step, side, c : c + 1, :]))
            place(left_back, side, senders_ref[side : side + 1, :], values)
        back = lax.dot_general(
            left_back[...], right_back[...], contract, preferred_element_type=jnp.float32
        )
        for c in range(3):
            base = 2 * c * table_rows
            own_force[c] = (
                own_force[c]
                + back[base : base + table_rows]
                + back[base + table_rows : base + 2 * table_rows]
            )

        height = 5 * SUB if modes % (5 * SUB) == 0 else SUB

        @pl.loop(0, modes // height)
        def _(b):
            rows = pl.ds(pl.multiple_of(b * height, SUB), height)
            acc = [None] * 3
            for c in range(3):
                for t in range(tiles):
                    term = phi[c, t, rows, :] * jnp.broadcast_to(
                        own_force[c, t : t + 1, :], (height, LANES)
                    )
                    acc[c] = term if acc[c] is None else acc[c] + term
            column[rows, :] = jnp.broadcast_to(
                jnp.sum(acc[0] + acc[1] + acc[2], axis=1, keepdims=True), (height, LANES)
            )

        for j in range(blocks):
            rows = min(LANES, modes - j * LANES)
            picked = jnp.where(eye[:rows], column[j * LANES : j * LANES + rows, :], 0.0)
            sum_x[step, ix, j : j + 1, :] = jnp.sum(picked, axis=0, keepdims=True)
        along_x, sent_x = total(step, sum_x, "gx", ix, n_x, x_send_sem, x_recv_sem)
        sum_y[step, iy] = along_x
        reduced, sent_y = total(step, sum_y, "gy", iy, n_y, y_send_sem, y_recv_sem)
        velocity = vectors[1] + time_step * (vectors[2] - reduced)
        vectors[3] = reduced
        vectors[1] = velocity
        vectors[0] = vectors[0] + time_step * velocity
        spread_coords()
        pl.loop(0, tiles)(displace)
        sent_u()
        sent_f()
        sent_x()
        sent_y()

    pl.loop(0, STEPS)(advance)

    for slot, ref in ((0, coords_out), (1, velocity_out), (3, reduced_out)):
        for j in range(blocks):
            width = min(LANES, modes - j * LANES)
            ref[:, j * LANES : j * LANES + width] = vectors[slot, j : j + 1, :width]
    for c in range(3):
        displaced_out[c * tiles : (c + 1) * tiles, :] = table[c, :tiles, :]


def shards(
    basis, connectivity, send_nodes, modulus, ecsw_weight, stiffness, coords, velocity, external
):
    modes, nodes = basis.shape[1], basis.shape[3]
    corners, elements = connectivity.shape[0], connectivity.shape[2]
    tiles, chunks = nodes // LANES, elements // LANES
    n_x, n_y = lax.axis_size("gx"), lax.axis_size("gy")
    blocks = pl.cdiv(modes, LANES)
    table_rows = pl.cdiv(tiles + 4, 16) * 16
    f32 = jnp.float32
    vmem = pl.BlockSpec(memory_space=pltpu.VMEM)
    tile = (SUB, LANES)
    dma = pltpu.SemaphoreType.DMA
    outs = pl.pallas_call(
        functools.partial(kernel, (modes, tiles, corners, chunks, n_x, n_y)),
        out_shape=[jax.ShapeDtypeStruct((1, modes), f32)] * 3
        + [jax.ShapeDtypeStruct((3 * tiles, LANES), f32)],
        in_specs=[pl.BlockSpec(memory_space=pl.ANY)]
        + [vmem] * 4
        + [pl.BlockSpec(memory_space=pltpu.SMEM)]
        + [vmem] * 3,
        out_specs=[vmem] * 4,
        scratch_shapes=[
            pltpu.VMEM((3, modes * tiles, LANES), f32),
            pltpu.VMEM((3, tiles, modes, LANES), f32),
            pltpu.VMEM((blocks * LANES, LANES), f32),
            pltpu.VMEM((4,) + tile, f32),
            pltpu.VMEM((3, table_rows, LANES), f32),
            pltpu.VMEM((chunks, LANES), f32),
            pltpu.VMEM((2, 3 * corners, chunks, LANES), f32),
            pltpu.VMEM((6 * table_rows, corners * elements), jnp.bfloat16),
            pltpu.VMEM((LANES, corners * elements), jnp.bfloat16),
            pltpu.VMEM((6 * table_rows, 4 * LANES), jnp.bfloat16),
            pltpu.VMEM((LANES, 4 * LANES), jnp.bfloat16),
            pltpu.VMEM((3, table_rows, LANES), f32),
            pltpu.VMEM((STEPS, 4) + tile, f32),
            pltpu.VMEM((STEPS, 4) + tile, f32),
            pltpu.VMEM((STEPS, 4) + tile, f32),
            pltpu.VMEM((STEPS, 4) + tile, f32),
            pltpu.VMEM((STEPS, n_x) + tile, f32),
            pltpu.VMEM((STEPS, n_y) + tile, f32),
            dma((3,)),
            dma((STEPS, 4)),
            dma((STEPS, 4)),
            dma((STEPS, 4)),
            dma((STEPS, 4)),
            dma((STEPS, n_x)),
            dma((STEPS, n_x)),
            dma((STEPS, n_y)),
            dma((STEPS, n_y)),
        ],
        compiler_params=pltpu.CompilerParams(collective_id=0, has_side_effects=True),
    )(
        basis.reshape(3 * modes * tiles, LANES),
        connectivity.reshape(corners * chunks, LANES),
        send_nodes.reshape(4, LANES),
        modulus.reshape(chunks, LANES),
        ecsw_weight.reshape(chunks, LANES),
        stiffness,
        coords.reshape(1, modes),
        velocity.reshape(1, modes),
        external.reshape(1, modes),
    )
    coords, velocity, reduced, displaced = outs
    return (
        coords.reshape(modes),
        velocity.reshape(modes),
        reduced.reshape(modes),
        displaced.reshape(3, 1, nodes),
    )


def solution(mesh):
    return jax.shard_map(
        shards,
        mesh=mesh,
        in_specs=(
            P(None, None, "gx", "gy"),
            P(None, "gx", "gy"),
            P(None, "gx", "gy"),
            P("gx", "gy"),
            P("gx", "gy"),
            P(),
            P(),
            P(),
            P(),
        ),
        out_specs=(P(), P(), P(), P(None, "gx", "gy")),
        check_vma=False,
    )
```

```python
import functools

import jax
import jax.numpy as jnp
from jax import lax
from jax.experimental import pallas as pl
from jax.experimental.pallas import tpu as pltpu
from jax.sharding import PartitionSpec as P

STEPS = 2
LANES = 128
SUB = 8

time_step = 0.05

MESH = pl.DeviceIdType.MESH


def split(x):
    high = x.astype(jnp.bfloat16).astype(jnp.float32)
    return high, x - high


def kernel(
    sizes,
    basis_hbm,
    links_ref,
    senders_ref,
    modulus_ref,
    weight_ref,
    stiffness_ref,
    coords_ref,
    velocity_ref,
    external_ref,
    packed_out,
    raw,
    phi,
    column,
    vectors,
    table,
    factor,
    moved,
    forces,
    left_hand,
    right_hand,
    left_back,
    right_back,
    own_force,
    send_u,
    recv_u,
    send_f,
    recv_f,
    sum_x,
    sum_y,
    load_sem,
    u_send_sem,
    u_recv_sem,
    f_send_sem,
    f_recv_sem,
    x_send_sem,
    x_recv_sem,
    y_send_sem,
    y_recv_sem,
):
    modes, tiles, corners, chunks, n_x, n_y = sizes
    blocks = pl.cdiv(modes, LANES)
    groups = own_force.shape[2]
    wide = right_hand.shape[0]
    ix = lax.axis_index("gx")
    iy = lax.axis_index("gy")

    loads = [
        pltpu.make_async_copy(
            basis_hbm.at[pl.ds(c * modes * tiles, modes * tiles), :], raw.at[c], load_sem.at[c]
        )
        for c in range(3)
    ]
    for load in loads:
        load.start()

    recv_u[...] = jnp.zeros_like(recv_u)
    recv_f[...] = jnp.zeros_like(recv_f)
    send_u[...] = jnp.zeros_like(send_u)
    send_f[...] = jnp.zeros_like(send_f)

    barrier = pltpu.get_barrier_semaphore()
    for d in range(1, n_x):
        pl.semaphore_signal(
            barrier, inc=1, device_id={"gx": lax.rem(ix + d, n_x)}, device_id_type=MESH
        )
    for d in range(1, n_y):
        pl.semaphore_signal(
            barrier, inc=1, device_id={"gy": lax.rem(iy + d, n_y)}, device_id_type=MESH
        )

    neighbours = [
        (ix > 0, {"gx": lax.rem(ix + n_x - 1, n_x)}),
        (ix < n_x - 1, {"gx": lax.rem(ix + 1, n_x)}),
        (iy > 0, {"gy": lax.rem(iy + n_y - 1, n_y)}),
        (iy < n_y - 1, {"gy": lax.rem(iy + 1, n_y)}),
    ]

    vectors[...] = jnp.zeros_like(vectors)
    for place, ref in enumerate((coords_ref, velocity_ref, external_ref)):
        for j in range(blocks):
            width = min(LANES, modes - j * LANES)
            vectors[place, j : j + 1, :width] = ref[:, j * LANES : j * LANES + width]

    lane = lax.broadcasted_iota(jnp.int32, (LANES, LANES), 1)
    sublane = lax.broadcasted_iota(jnp.int32, (LANES, LANES), 0)
    eye = lane == sublane

    def spread_coords():
        for j in range(blocks):
            height = min(LANES, modes - j * LANES)
            row = jnp.broadcast_to(vectors[0, j : j + 1, :], (height, LANES))
            picked = jnp.where(eye[:height], row, 0.0)
            column[j * LANES : j * LANES + height, :] = jnp.broadcast_to(
                jnp.sum(picked, axis=1, keepdims=True), (height, LANES)
            )

    def fold(product):
        parts = [product[SUB * i : SUB * (i + 1)] for i in range(modes // SUB)]
        while len(parts) > 1:
            nxt = [parts[i] + parts[i + 1] for i in range(0, len(parts) - 1, 2)]
            if len(parts) % 2:
                nxt.append(parts[-1])
            parts = nxt
        return jnp.sum(parts[0], axis=0, keepdims=True)

    def move_tile(t, c):
        rows = raw[c, pl.ds(t, modes, stride=tiles), :]
        phi[c, t] = rows
        table[c, pl.ds(t, 1), :] = fold(rows * column[:modes, :])

    def displace(t):
        spread = column[:modes, :]
        for c in range(3):
            table[c, pl.ds(t, 1), :] = fold(phi[c, t] * spread)

    low_rows = lax.broadcasted_iota(jnp.int32, (wide, LANES), 0)

    def one_hot(target, chunk, index):
        low = jnp.broadcast_to(index & (wide - 1), (wide, LANES))
        target[:, chunk * LANES : (chunk + 1) * LANES] = jnp.where(
            low == low_rows, 1.0, 0.0
        ).astype(jnp.bfloat16)

    def prepare():
        for chunk in range(corners * chunks):
            one_hot(right_hand, chunk, links_ref[chunk : chunk + 1, :])
        for side in range(4):
            one_hot(right_back, side, senders_ref[side : side + 1, :])

    factor[...] = modulus_ref[...] * weight_ref[...]
    spread_coords()

    for c in range(3):
        loads[c].wait()
        pl.loop(0, tiles)(functools.partial(move_tile, c=c))

    pl.semaphore_wait(barrier, n_x + n_y - 2)

    high_rows = lax.broadcasted_iota(jnp.int32, (groups, LANES), 0)
    contract = (((1,), (1,)), ((), ()))

    def exchange(step, source, target, send_sem, recv_sem):
        copies = []
        for side, (exists, where) in enumerate(neighbours):
            copies.append(
                pltpu.make_async_remote_copy(
                    src_ref=source.at[step, side],
                    dst_ref=target.at[step, side ^ 1],
                    send_sem=send_sem.at[step, side],
                    recv_sem=recv_sem.at[step, side ^ 1],
                    device_id=where,
                    device_id_type=MESH,
                )
            )
        for side, (exists, where) in enumerate(neighbours):
            pl.when(exists)(copies[side].start)
        return copies

    def arrive(step, source, target, send_sem, recv_sem):
        for side, (exists, where) in enumerate(neighbours):
            arrived = pltpu.make_async_remote_copy(
                src_ref=source.at[step, side],
                dst_ref=target.at[step, side],
                send_sem=send_sem.at[step, side],
                recv_sem=recv_sem.at[step, side],
                device_id=where,
                device_id_type=MESH,
            )
            pl.when(exists)(arrived.wait_recv)

    def sent(copies):
        for side, (exists, where) in enumerate(neighbours):
            pl.when(exists)(copies[side].wait_send)

    def total(step, slots, axis, me, size, send_sem, recv_sem):
        copies = []
        for d in range(1, size):
            copies.append(
                pltpu.make_async_remote_copy(
                    src_ref=slots.at[step, me],
                    dst_ref=slots.at[step, me],
                    send_sem=send_sem.at[step, d],
                    recv_sem=recv_sem.at[step, me],
                    device_id={axis: lax.rem(me + d, size)},
                    device_id_type=MESH,
                )
            )
            copies[-1].start()
        for d in range(1, size):
            other = lax.rem(me + d, size)
            pltpu.make_async_remote_copy(
                src_ref=slots.at[step, other],
                dst_ref=slots.at[step, other],
                send_sem=send_sem.at[step, d],
                recv_sem=recv_sem.at[step, other],
                device_id={axis: other},
                device_id_type=MESH,
            ).wait_recv()
        value = slots[step, 0]
        for i in range(1, size):
            value = value + slots[step, i]
        return value, lambda: [copy.wait_send() for copy in copies]

    def gather(index, rows, found):
        low = index & (LANES - 1)
        high = lax.shift_right_logical(index, 7)
        for r, row_of in rows:
            here = high == r
            for c in range(3):
                row = jnp.broadcast_to(row_of(c), index.shape)
                taken = jnp.take_along_axis(row, low, axis=1, mode="promise_in_bounds")
                found[c] = jnp.where(here, taken, found[c])
        return found

    own_rows = [(r, lambda c, r=r: table[c, r : r + 1, :]) for r in range(tiles)]
    senders = jnp.concatenate([senders_ref[...], jnp.zeros((4, LANES), jnp.int32)], axis=0)
    zero = jnp.zeros((chunks, LANES), jnp.float32)

    def place(target, chunk, index, values):
        here = jnp.broadcast_to(lax.shift_right_logical(index, 8), high_rows.shape) == high_rows
        for c, pair in enumerate(values):
            both = [jnp.where(here, jnp.broadcast_to(x, high_rows.shape), 0.0) for x in pair]
            target[2 * c * groups : 2 * (c + 1) * groups, chunk * LANES : (chunk + 1) * LANES] = (
                jnp.concatenate(both, axis=0).astype(jnp.bfloat16)
            )

    def scattered(left, right):
        product = lax.dot_general(
            left[...], right[...], contract, preferred_element_type=jnp.float32
        )
        return [
            product[2 * c * groups : (2 * c + 1) * groups]
            + product[(2 * c + 1) * groups : (2 * c + 2) * groups]
            for c in range(3)
        ]

    def advance(step):
        for c, found in enumerate(
            gather(senders, own_rows, [jnp.zeros((SUB, LANES), jnp.float32)] * 3)
        ):
            for side in range(4):
                send_u[step, side, c : c + 1, :] = found[side : side + 1, :]
        sent_u = exchange(step, send_u, recv_u, u_send_sem, u_recv_sem)
        pl.when(step == 0)(prepare)
        for q in range(corners):
            index = links_ref[q * chunks : (q + 1) * chunks, :]
            for c, found in enumerate(gather(index, own_rows, [zero] * 3)):
                moved[c * corners + q] = found
        arrive(step, send_u, recv_u, u_send_sem, u_recv_sem)
        edge_rows = [
            (tiles + side, lambda c, side=side: recv_u[step, side, c : c + 1, :])
            for side in range(4)
        ]
        corner = [None] * (3 * corners)
        for q in range(corners):
            index = links_ref[q * chunks : (q + 1) * chunks, :]
            begun = [moved[c * corners + q] for c in range(3)]
            for c, found in enumerate(gather(index, edge_rows, begun)):
                corner[c * corners + q] = found
        for i in range(3 * corners):
            strain = stiffness_ref[i, 0] * corner[0]
            for j in range(1, 3 * corners):
                strain = strain + stiffness_ref[i, j] * corner[j]
            force = factor[...] * (strain + strain * strain * strain * (1.0 / 3.0))
            forces[0, i], forces[1, i] = split(force)
        for q in range(corners):
            for s in range(chunks):
                chunk = q * chunks + s
                place(
                    left_hand,
                    chunk,
                    links_ref[chunk : chunk + 1, :],
                    [
                        [forces[h, c * corners + q, s : s + 1, :] for h in range(2)]
                        for c in range(3)
                    ],
                )
        for c, both in enumerate(scattered(left_hand, right_hand)):
            for half in range(2):
                own_force[c, half] = both[:, half * LANES : (half + 1) * LANES]
            for side in range(4):
                row, half = (tiles + side) // 2, (tiles + side) % 2
                send_f[step, side, c : c + 1, :] = both[
                    row : row + 1, half * LANES : (half + 1) * LANES
                ]
        sent_f = exchange(step, send_f, recv_f, f_send_sem, f_recv_sem)
        arrive(step, send_f, recv_f, f_send_sem, f_recv_sem)
        for side in range(4):
            place(
                left_back,
                side,
                senders_ref[side : side + 1, :],
                [split(recv_f[step, side, c : c + 1, :]) for c in range(3)],
            )
        for c, both in enumerate(scattered(left_back, right_back)):
            for half in range(2):
                own_force[c, half] += both[:, half * LANES : (half + 1) * LANES]

        height = 5 * SUB if modes % (5 * SUB) == 0 else SUB

        @pl.loop(0, modes // height)
        def _(b):
            rows = pl.ds(pl.multiple_of(b * height, SUB), height)
            acc = [None] * 3
            for c in range(3):
                for t in range(tiles):
                    term = phi[c, t, rows, :] * jnp.broadcast_to(
                        own_force[c, t % 2, t // 2 : t // 2 + 1, :], (height, LANES)
                    )
                    acc[c] = term if acc[c] is None else acc[c] + term
            column[rows, :] = jnp.broadcast_to(
                jnp.sum(acc[0] + acc[1] + acc[2], axis=1, keepdims=True), (height, LANES)
            )

        for j in range(blocks):
            rows = min(LANES, modes - j * LANES)
            picked = jnp.where(eye[:rows], column[j * LANES : j * LANES + rows, :], 0.0)
            sum_x[step, ix, j : j + 1, :] = jnp.sum(picked, axis=0, keepdims=True)
        along_x, sent_x = total(step, sum_x, "gx", ix, n_x, x_send_sem, x_recv_sem)
        sum_y[step, iy] = along_x
        reduced, sent_y = total(step, sum_y, "gy", iy, n_y, y_send_sem, y_recv_sem)
        velocity = vectors[1] + time_step * (vectors[2] - reduced)
        vectors[3] = reduced
        vectors[1] = velocity
        vectors[0] = vectors[0] + time_step * velocity
        spread_coords()
        pl.loop(0, tiles)(displace)
        sent(sent_u)
        sent(sent_f)
        sent_x()
        sent_y()

    pl.loop(0, STEPS)(advance)

    for place_out, slot in enumerate((0, 1, 3)):
        packed_out[place_out * blocks : (place_out + 1) * blocks, :] = vectors[slot]
    for c in range(3):
        first = 3 * blocks + c * tiles
        packed_out[first : first + tiles, :] = table[c, :tiles, :]


def unpack(packed, coords_out, velocity_out, reduced_out, displaced_out):
    modes = coords_out.shape[1]
    blocks = pl.cdiv(modes, LANES)
    for slot, ref in enumerate((coords_out, velocity_out, reduced_out)):
        for j in range(blocks):
            width = min(LANES, modes - j * LANES)
            row = slot * blocks + j
            ref[:, j * LANES : j * LANES + width] = packed[row : row + 1, :width]
    tiles = displaced_out.shape[2] // LANES
    for c in range(3):
        for t in range(tiles):
            row = 3 * blocks + c * tiles + t
            displaced_out[c, :, t * LANES : (t + 1) * LANES] = packed[row : row + 1, :]


def shards(
    basis, connectivity, send_nodes, modulus, ecsw_weight, stiffness, coords, velocity, external
):
    modes, nodes = basis.shape[1], basis.shape[3]
    corners, elements = connectivity.shape[0], connectivity.shape[2]
    tiles, chunks = nodes // LANES, elements // LANES
    n_x, n_y = lax.axis_size("gx"), lax.axis_size("gy")
    blocks = pl.cdiv(modes, LANES)
    groups = pl.cdiv(pl.cdiv(tiles + 4, 2), SUB) * SUB
    wide = 2 * LANES
    f32 = jnp.float32
    vmem = pl.BlockSpec(memory_space=pltpu.VMEM)
    tile = (4, LANES)
    dma = pltpu.SemaphoreType.DMA
    packed = pl.pallas_call(
        functools.partial(kernel, (modes, tiles, corners, chunks, n_x, n_y)),
        out_shape=jax.ShapeDtypeStruct((3 * blocks + 3 * tiles, LANES), f32),
        in_specs=[pl.BlockSpec(memory_space=pl.ANY)]
        + [vmem] * 4
        + [pl.BlockSpec(memory_space=pltpu.SMEM)]
        + [vmem] * 3,
        out_specs=vmem,
        scratch_shapes=[
            pltpu.VMEM((3, modes * tiles, LANES), f32),
            pltpu.VMEM((3, tiles, modes, LANES), f32),
            pltpu.VMEM((blocks * LANES, LANES), f32),
            pltpu.VMEM((4, blocks, LANES), f32),
            pltpu.VMEM((3, tiles, LANES), f32),
            pltpu.VMEM((chunks, LANES), f32),
            pltpu.VMEM((3 * corners, chunks, LANES), f32),
            pltpu.VMEM((2, 3 * corners, chunks, LANES), f32),
            pltpu.VMEM((6 * groups, corners * elements), jnp.bfloat16),
            pltpu.VMEM((wide, corners * elements), jnp.bfloat16),
            pltpu.VMEM((6 * groups, 4 * LANES), jnp.bfloat16),
            pltpu.VMEM((wide, 4 * LANES), jnp.bfloat16),
            pltpu.VMEM((3, 2, groups, LANES), f32),
            pltpu.VMEM((STEPS, 4) + tile, f32),
            pltpu.VMEM((STEPS, 4) + tile, f32),
            pltpu.VMEM((STEPS, 4) + tile, f32),
            pltpu.VMEM((STEPS, 4) + tile, f32),
            pltpu.VMEM((STEPS, n_x, blocks, LANES), f32),
            pltpu.VMEM((STEPS, n_y, blocks, LANES), f32),
            dma((3,)),
            dma((STEPS, 4)),
            dma((STEPS, 4)),
            dma((STEPS, 4)),
            dma((STEPS, 4)),
            dma((STEPS, n_x)),
            dma((STEPS, n_x)),
            dma((STEPS, n_y)),
            dma((STEPS, n_y)),
        ],
        compiler_params=pltpu.CompilerParams(collective_id=0, has_side_effects=True),
    )(
        basis.reshape(3 * modes * tiles, LANES),
        connectivity.reshape(corners * chunks, LANES),
        send_nodes.reshape(4, LANES),
        modulus.reshape(chunks, LANES),
        ecsw_weight.reshape(chunks, LANES),
        stiffness,
        coords.reshape(1, modes),
        velocity.reshape(1, modes),
        external.reshape(1, modes),
    )
    coords, velocity, reduced, displaced = pl.pallas_call(
        unpack,
        out_shape=[jax.ShapeDtypeStruct((1, modes), f32)] * 3
        + [jax.ShapeDtypeStruct((3, 1, nodes), f32)],
        in_specs=[vmem],
        out_specs=[vmem] * 4,
    )(packed)
    return (
        coords.reshape(modes),
        velocity.reshape(modes),
        reduced.reshape(modes),
        displaced,
    )


def solution(mesh):
    return jax.shard_map(
        shards,
        mesh=mesh,
        in_specs=(
            P(None, None, "gx", "gy"),
            P(None, "gx", "gy"),
            P(None, "gx", "gy"),
            P("gx", "gy"),
            P("gx", "gy"),
            P(),
            P(),
            P(),
            P(),
        ),
        out_specs=(P(), P(), P(), P(None, "gx", "gy")),
        check_vma=False,
    )
```

```python
import functools

import jax
import jax.numpy as jnp
from jax import lax
from jax.experimental import pallas as pl
from jax.experimental.pallas import tpu as pltpu
from jax.sharding import PartitionSpec as P

STEPS = 2
LANES = 128
SUB = 8

time_step = 0.05

MESH = pl.DeviceIdType.MESH


def split(x):
    high = x.astype(jnp.bfloat16).astype(jnp.float32)
    return high, x - high


def kernel(
    sizes,
    basis_hbm,
    links_hbm,
    senders_hbm,
    modulus_hbm,
    weight_hbm,
    stiffness_hbm,
    coords_hbm,
    velocity_hbm,
    external_hbm,
    packed_out,
    links_ref,
    senders_ref,
    modulus_ref,
    weight_ref,
    stiffness_ref,
    coords_ref,
    velocity_ref,
    external_ref,
    small_sem,
    raw,
    phi,
    column,
    vectors,
    table,
    factor,
    moved,
    forces,
    left_hand,
    right_hand,
    left_back,
    right_back,
    own_force,
    send_u,
    recv_u,
    send_f,
    recv_f,
    sum_x,
    sum_y,
    load_sem,
    u_send_sem,
    u_recv_sem,
    f_send_sem,
    f_recv_sem,
    x_send_sem,
    x_recv_sem,
    y_send_sem,
    y_recv_sem,
):
    modes, tiles, corners, chunks, n_x, n_y = sizes
    blocks = pl.cdiv(modes, LANES)
    groups = own_force.shape[2]
    wide = right_hand.shape[0]
    ix = lax.axis_index("gx")
    iy = lax.axis_index("gy")

    loads = [
        pltpu.make_async_copy(
            basis_hbm.at[pl.ds(c * modes * tiles, modes * tiles), :], raw.at[c], load_sem.at[c]
        )
        for c in range(3)
    ]
    recv_u[...] = jnp.zeros_like(recv_u)
    recv_f[...] = jnp.zeros_like(recv_f)

    barrier = pltpu.get_barrier_semaphore()
    for d in range(1, n_x):
        pl.semaphore_signal(
            barrier, inc=1, device_id={"gx": lax.rem(ix + d, n_x)}, device_id_type=MESH
        )
    for d in range(1, n_y):
        pl.semaphore_signal(
            barrier, inc=1, device_id={"gy": lax.rem(iy + d, n_y)}, device_id_type=MESH
        )

    small = [
        pltpu.make_async_copy(source, target, small_sem.at[i])
        for i, (source, target) in enumerate(
            (
                (coords_hbm, coords_ref),
                (velocity_hbm, velocity_ref),
                (external_hbm, external_ref),
                (senders_hbm, senders_ref),
                (links_hbm, links_ref),
                (modulus_hbm, modulus_ref),
                (weight_hbm, weight_ref),
                (stiffness_hbm, stiffness_ref),
            )
        )
    ]
    for load in small + loads:
        load.start()
    send_u[...] = jnp.zeros_like(send_u)
    send_f[...] = jnp.zeros_like(send_f)

    neighbours = [
        (ix > 0, {"gx": lax.rem(ix + n_x - 1, n_x)}),
        (ix < n_x - 1, {"gx": lax.rem(ix + 1, n_x)}),
        (iy > 0, {"gy": lax.rem(iy + n_y - 1, n_y)}),
        (iy < n_y - 1, {"gy": lax.rem(iy + 1, n_y)}),
    ]

    vectors[...] = jnp.zeros_like(vectors)
    for load in small:
        load.wait()
    for place, ref in enumerate((coords_ref, velocity_ref, external_ref)):
        for j in range(blocks):
            width = min(LANES, modes - j * LANES)
            vectors[place, j : j + 1, :width] = ref[:, j * LANES : j * LANES + width]

    lane = lax.broadcasted_iota(jnp.int32, (LANES, LANES), 1)
    sublane = lax.broadcasted_iota(jnp.int32, (LANES, LANES), 0)
    eye = lane == sublane

    def spread_coords():
        for j in range(blocks):
            height = min(LANES, modes - j * LANES)
            row = jnp.broadcast_to(vectors[0, j : j + 1, :], (height, LANES))
            picked = jnp.where(eye[:height], row, 0.0)
            column[j * LANES : j * LANES + height, :] = jnp.broadcast_to(
                jnp.sum(picked, axis=1, keepdims=True), (height, LANES)
            )

    def fold(product):
        parts = [product[SUB * i : SUB * (i + 1)] for i in range(modes // SUB)]
        while len(parts) > 1:
            nxt = [parts[i] + parts[i + 1] for i in range(0, len(parts) - 1, 2)]
            if len(parts) % 2:
                nxt.append(parts[-1])
            parts = nxt
        return jnp.sum(parts[0], axis=0, keepdims=True)

    def move_tile(t, c):
        rows = raw[c, pl.ds(t, modes, stride=tiles), :]
        phi[c, t] = rows
        table[c, pl.ds(t, 1), :] = fold(rows * column[:modes, :])

    def displace(t):
        spread = column[:modes, :]
        for c in range(3):
            table[c, pl.ds(t, 1), :] = fold(phi[c, t] * spread)

    low_rows = lax.broadcasted_iota(jnp.int32, (wide, LANES), 0)

    def one_hot(target, chunk, index):
        low = jnp.broadcast_to(index & (wide - 1), (wide, LANES))
        target[:, chunk * LANES : (chunk + 1) * LANES] = jnp.where(
            low == low_rows, 1.0, 0.0
        ).astype(jnp.bfloat16)

    def prepare():
        for chunk in range(corners * chunks):
            one_hot(right_hand, chunk, links_ref[chunk : chunk + 1, :])
        for side in range(4):
            one_hot(right_back, side, senders_ref[side : side + 1, :])

    factor[...] = modulus_ref[...] * weight_ref[...]
    spread_coords()

    for c in range(3):
        loads[c].wait()
        pl.loop(0, tiles)(functools.partial(move_tile, c=c))

    pl.semaphore_wait(barrier, n_x + n_y - 2)

    high_rows = lax.broadcasted_iota(jnp.int32, (groups, LANES), 0)
    contract = (((1,), (1,)), ((), ()))

    def exchange(step, source, target, send_sem, recv_sem):
        copies = []
        for side, (exists, where) in enumerate(neighbours):
            copies.append(
                pltpu.make_async_remote_copy(
                    src_ref=source.at[step, side],
                    dst_ref=target.at[step, side ^ 1],
                    send_sem=send_sem.at[step, side],
                    recv_sem=recv_sem.at[step, side ^ 1],
                    device_id=where,
                    device_id_type=MESH,
                )
            )
        for side, (exists, where) in enumerate(neighbours):
            pl.when(exists)(copies[side].start)
        return copies

    def arrive(step, source, target, send_sem, recv_sem):
        for side, (exists, where) in enumerate(neighbours):
            arrived = pltpu.make_async_remote_copy(
                src_ref=source.at[step, side],
                dst_ref=target.at[step, side],
                send_sem=send_sem.at[step, side],
                recv_sem=recv_sem.at[step, side],
                device_id=where,
                device_id_type=MESH,
            )
            pl.when(exists)(arrived.wait_recv)

    def sent(copies):
        for side, (exists, where) in enumerate(neighbours):
            pl.when(exists)(copies[side].wait_send)

    def total(step, slots, axis, me, size, send_sem, recv_sem):
        copies = []
        for d in range(1, size):
            copies.append(
                pltpu.make_async_remote_copy(
                    src_ref=slots.at[step, me],
                    dst_ref=slots.at[step, me],
                    send_sem=send_sem.at[step, d],
                    recv_sem=recv_sem.at[step, me],
                    device_id={axis: lax.rem(me + d, size)},
                    device_id_type=MESH,
                )
            )
            copies[-1].start()
        for d in range(1, size):
            other = lax.rem(me + d, size)
            pltpu.make_async_remote_copy(
                src_ref=slots.at[step, other],
                dst_ref=slots.at[step, other],
                send_sem=send_sem.at[step, d],
                recv_sem=recv_sem.at[step, other],
                device_id={axis: other},
                device_id_type=MESH,
            ).wait_recv()
        value = slots[step, 0]
        for i in range(1, size):
            value = value + slots[step, i]
        return value, lambda: [copy.wait_send() for copy in copies]

    def gather(index, rows, found):
        low = index & (LANES - 1)
        high = lax.shift_right_logical(index, 7)
        for r, row_of in rows:
            here = high == r
            for c in range(3):
                row = jnp.broadcast_to(row_of(c), index.shape)
                taken = jnp.take_along_axis(row, low, axis=1, mode="promise_in_bounds")
                found[c] = jnp.where(here, taken, found[c])
        return found

    own_rows = [(r, lambda c, r=r: table[c, r : r + 1, :]) for r in range(tiles)]
    senders = jnp.concatenate([senders_ref[...], jnp.zeros((4, LANES), jnp.int32)], axis=0)
    zero = jnp.zeros((chunks, LANES), jnp.float32)

    def place(target, chunk, index, values):
        here = jnp.broadcast_to(lax.shift_right_logical(index, 8), high_rows.shape) == high_rows
        for c, pair in enumerate(values):
            both = [jnp.where(here, jnp.broadcast_to(x, high_rows.shape), 0.0) for x in pair]
            target[2 * c * groups : 2 * (c + 1) * groups, chunk * LANES : (chunk + 1) * LANES] = (
                jnp.concatenate(both, axis=0).astype(jnp.bfloat16)
            )

    def scattered(left, right):
        product = lax.dot_general(
            left[...], right[...], contract, preferred_element_type=jnp.float32
        )
        return [
            product[2 * c * groups : (2 * c + 1) * groups]
            + product[(2 * c + 1) * groups : (2 * c + 2) * groups]
            for c in range(3)
        ]

    def advance(step):
        for c, found in enumerate(
            gather(senders, own_rows, [jnp.zeros((SUB, LANES), jnp.float32)] * 3)
        ):
            for side in range(4):
                send_u[step, side, c : c + 1, :] = found[side : side + 1, :]
        sent_u = exchange(step, send_u, recv_u, u_send_sem, u_recv_sem)
        pl.when(step == 0)(prepare)
        for q in range(corners):
            index = links_ref[q * chunks : (q + 1) * chunks, :]
            for c, found in enumerate(gather(index, own_rows, [zero] * 3)):
                moved[c * corners + q] = found
        arrive(step, send_u, recv_u, u_send_sem, u_recv_sem)
        edge_rows = [
            (tiles + side, lambda c, side=side: recv_u[step, side, c : c + 1, :])
            for side in range(4)
        ]
        corner = [None] * (3 * corners)
        for q in range(corners):
            index = links_ref[q * chunks : (q + 1) * chunks, :]
            begun = [moved[c * corners + q] for c in range(3)]
            for c, found in enumerate(gather(index, edge_rows, begun)):
                corner[c * corners + q] = found
        for i in range(3 * corners):
            strain = stiffness_ref[i, 0] * corner[0]
            for j in range(1, 3 * corners):
                strain = strain + stiffness_ref[i, j] * corner[j]
            force = factor[...] * (strain + strain * strain * strain * (1.0 / 3.0))
            forces[0, i], forces[1, i] = split(force)
        for q in range(corners):
            for s in range(chunks):
                chunk = q * chunks + s
                place(
                    left_hand,
                    chunk,
                    links_ref[chunk : chunk + 1, :],
                    [
                        [forces[h, c * corners + q, s : s + 1, :] for h in range(2)]
                        for c in range(3)
                    ],
                )
        for c, both in enumerate(scattered(left_hand, right_hand)):
            for half in range(2):
                own_force[c, half] = both[:, half * LANES : (half + 1) * LANES]
            for side in range(4):
                row, half = (tiles + side) // 2, (tiles + side) % 2
                send_f[step, side, c : c + 1, :] = both[
                    row : row + 1, half * LANES : (half + 1) * LANES
                ]
        sent_f = exchange(step, send_f, recv_f, f_send_sem, f_recv_sem)
        arrive(step, send_f, recv_f, f_send_sem, f_recv_sem)
        for side in range(4):
            place(
                left_back,
                side,
                senders_ref[side : side + 1, :],
                [split(recv_f[step, side, c : c + 1, :]) for c in range(3)],
            )
        for c, both in enumerate(scattered(left_back, right_back)):
            for half in range(2):
                own_force[c, half] += both[:, half * LANES : (half + 1) * LANES]

        height = 5 * SUB if modes % (5 * SUB) == 0 else SUB

        @pl.loop(0, modes // height)
        def _(b):
            rows = pl.ds(pl.multiple_of(b * height, SUB), height)
            acc = [None] * 3
            for c in range(3):
                for t in range(tiles):
                    term = phi[c, t, rows, :] * jnp.broadcast_to(
                        own_force[c, t % 2, t // 2 : t // 2 + 1, :], (height, LANES)
                    )
                    acc[c] = term if acc[c] is None else acc[c] + term
            column[rows, :] = jnp.broadcast_to(
                jnp.sum(acc[0] + acc[1] + acc[2], axis=1, keepdims=True), (height, LANES)
            )

        for j in range(blocks):
            rows = min(LANES, modes - j * LANES)
            picked = jnp.where(eye[:rows], column[j * LANES : j * LANES + rows, :], 0.0)
            sum_x[step, ix, j : j + 1, :] = jnp.sum(picked, axis=0, keepdims=True)
        along_x, sent_x = total(step, sum_x, "gx", ix, n_x, x_send_sem, x_recv_sem)
        sum_y[step, iy] = along_x
        reduced, sent_y = total(step, sum_y, "gy", iy, n_y, y_send_sem, y_recv_sem)
        velocity = vectors[1] + time_step * (vectors[2] - reduced)
        vectors[3] = reduced
        vectors[1] = velocity
        vectors[0] = vectors[0] + time_step * velocity
        spread_coords()
        pl.loop(0, tiles)(displace)
        sent(sent_u)
        sent(sent_f)
        sent_x()
        sent_y()

    pl.loop(0, STEPS)(advance)

    for place_out, slot in enumerate((0, 1, 3)):
        packed_out[place_out * blocks : (place_out + 1) * blocks, :] = vectors[slot]
    for c in range(3):
        first = 3 * blocks + c * tiles
        packed_out[first : first + tiles, :] = table[c, :tiles, :]


def unpack(packed, coords_out, velocity_out, reduced_out, displaced_out):
    modes = coords_out.shape[1]
    blocks = pl.cdiv(modes, LANES)
    for slot, ref in enumerate((coords_out, velocity_out, reduced_out)):
        for j in range(blocks):
            width = min(LANES, modes - j * LANES)
            row = slot * blocks + j
            ref[:, j * LANES : j * LANES + width] = packed[row : row + 1, :width]
    tiles = displaced_out.shape[2] // LANES
    for c in range(3):
        for t in range(tiles):
            row = 3 * blocks + c * tiles + t
            displaced_out[c, :, t * LANES : (t + 1) * LANES] = packed[row : row + 1, :]


def shards(
    basis, connectivity, send_nodes, modulus, ecsw_weight, stiffness, coords, velocity, external
):
    modes, nodes = basis.shape[1], basis.shape[3]
    corners, elements = connectivity.shape[0], connectivity.shape[2]
    tiles, chunks = nodes // LANES, elements // LANES
    n_x, n_y = lax.axis_size("gx"), lax.axis_size("gy")
    blocks = pl.cdiv(modes, LANES)
    groups = pl.cdiv(pl.cdiv(tiles + 4, 2), SUB) * SUB
    wide = 2 * LANES
    f32 = jnp.float32
    vmem = pl.BlockSpec(memory_space=pltpu.VMEM)
    tile = (4, LANES)
    dma = pltpu.SemaphoreType.DMA
    packed = pl.pallas_call(
        functools.partial(kernel, (modes, tiles, corners, chunks, n_x, n_y)),
        out_shape=jax.ShapeDtypeStruct((3 * blocks + 3 * tiles, LANES), f32),
        in_specs=[pl.BlockSpec(memory_space=pl.ANY)] * 9,
        out_specs=vmem,
        scratch_shapes=[
            pltpu.VMEM((corners * chunks, LANES), jnp.int32),
            pltpu.VMEM((4, LANES), jnp.int32),
            pltpu.VMEM((chunks, LANES), f32),
            pltpu.VMEM((chunks, LANES), f32),
            pltpu.SMEM(stiffness.shape, f32),
            pltpu.VMEM((1, modes), f32),
            pltpu.VMEM((1, modes), f32),
            pltpu.VMEM((1, modes), f32),
            dma((8,)),
            pltpu.VMEM((3, modes * tiles, LANES), f32),
            pltpu.VMEM((3, tiles, modes, LANES), f32),
            pltpu.VMEM((blocks * LANES, LANES), f32),
            pltpu.VMEM((4, blocks, LANES), f32),
            pltpu.VMEM((3, tiles, LANES), f32),
            pltpu.VMEM((chunks, LANES), f32),
            pltpu.VMEM((3 * corners, chunks, LANES), f32),
            pltpu.VMEM((2, 3 * corners, chunks, LANES), f32),
            pltpu.VMEM((6 * groups, corners * elements), jnp.bfloat16),
            pltpu.VMEM((wide, corners * elements), jnp.bfloat16),
            pltpu.VMEM((6 * groups, 4 * LANES), jnp.bfloat16),
            pltpu.VMEM((wide, 4 * LANES), jnp.bfloat16),
            pltpu.VMEM((3, 2, groups, LANES), f32),
            pltpu.VMEM((STEPS, 4) + tile, f32),
            pltpu.VMEM((STEPS, 4) + tile, f32),
            pltpu.VMEM((STEPS, 4) + tile, f32),
            pltpu.VMEM((STEPS, 4) + tile, f32),
            pltpu.VMEM((STEPS, n_x, blocks, LANES), f32),
            pltpu.VMEM((STEPS, n_y, blocks, LANES), f32),
            dma((3,)),
            dma((STEPS, 4)),
            dma((STEPS, 4)),
            dma((STEPS, 4)),
            dma((STEPS, 4)),
            dma((STEPS, n_x)),
            dma((STEPS, n_x)),
            dma((STEPS, n_y)),
            dma((STEPS, n_y)),
        ],
        compiler_params=pltpu.CompilerParams(collective_id=0, has_side_effects=True),
    )(
        basis.reshape(3 * modes * tiles, LANES),
        connectivity.reshape(corners * chunks, LANES),
        send_nodes.reshape(4, LANES),
        modulus.reshape(chunks, LANES),
        ecsw_weight.reshape(chunks, LANES),
        stiffness,
        coords.reshape(1, modes),
        velocity.reshape(1, modes),
        external.reshape(1, modes),
    )
    coords, velocity, reduced, displaced = pl.pallas_call(
        unpack,
        out_shape=[jax.ShapeDtypeStruct((1, modes), f32)] * 3
        + [jax.ShapeDtypeStruct((3, 1, nodes), f32)],
        in_specs=[vmem],
        out_specs=[vmem] * 4,
    )(packed)
    return (
        coords.reshape(modes),
        velocity.reshape(modes),
        reduced.reshape(modes),
        displaced,
    )


def solution(mesh):
    return jax.shard_map(
        shards,
        mesh=mesh,
        in_specs=(
            P(None, None, "gx", "gy"),
            P(None, "gx", "gy"),
            P(None, "gx", "gy"),
            P("gx", "gy"),
            P("gx", "gy"),
            P(),
            P(),
            P(),
            P(),
        ),
        out_specs=(P(), P(), P(), P(None, "gx", "gy")),
        check_vma=False,
    )
```

```python
import functools

import jax
import jax.numpy as jnp
from jax import lax
from jax.experimental import pallas as pl
from jax.experimental.pallas import tpu as pltpu
from jax.sharding import PartitionSpec as P

STEPS = 2
LANES = 128
SUB = 8

time_step = 0.05

MESH = pl.DeviceIdType.MESH


def split(x):
    high = x.astype(jnp.bfloat16).astype(jnp.float32)
    return high, x - high


def kernel(
    sizes,
    basis_hbm,
    links_hbm,
    senders_hbm,
    modulus_hbm,
    weight_hbm,
    stiffness_hbm,
    coords_hbm,
    velocity_hbm,
    external_hbm,
    packed_out,
    links_ref,
    senders_ref,
    modulus_ref,
    weight_ref,
    stiffness_ref,
    coords_ref,
    velocity_ref,
    external_ref,
    small_sem,
    raw,
    phi,
    column,
    vectors,
    table,
    factor,
    moved,
    forces,
    left_hand,
    right_hand,
    left_back,
    right_back,
    own_force,
    send_u,
    recv_u,
    send_f,
    recv_f,
    sum_x,
    sum_y,
    load_sem,
    u_send_sem,
    u_recv_sem,
    f_send_sem,
    f_recv_sem,
    x_send_sem,
    x_recv_sem,
    y_send_sem,
    y_recv_sem,
):
    modes, tiles, corners, chunks, n_x, n_y = sizes
    blocks = pl.cdiv(modes, LANES)
    groups = own_force.shape[2]
    wide = right_hand.shape[0]
    ix = lax.axis_index("gx")
    iy = lax.axis_index("gy")

    loads = [
        pltpu.make_async_copy(
            basis_hbm.at[pl.ds(c * modes * tiles, modes * tiles), :], raw.at[c], load_sem.at[c]
        )
        for c in range(3)
    ]
    recv_u[...] = jnp.zeros_like(recv_u)
    recv_f[...] = jnp.zeros_like(recv_f)

    barrier = pltpu.get_barrier_semaphore()
    for d in range(1, n_x):
        pl.semaphore_signal(
            barrier, inc=1, device_id={"gx": lax.rem(ix + d, n_x)}, device_id_type=MESH
        )
    for d in range(1, n_y):
        pl.semaphore_signal(
            barrier, inc=1, device_id={"gy": lax.rem(iy + d, n_y)}, device_id_type=MESH
        )

    small = [
        pltpu.make_async_copy(source, target, small_sem.at[i])
        for i, (source, target) in enumerate(
            (
                (coords_hbm, coords_ref),
                (velocity_hbm, velocity_ref),
                (external_hbm, external_ref),
                (senders_hbm, senders_ref),
                (links_hbm, links_ref),
                (modulus_hbm, modulus_ref),
                (weight_hbm, weight_ref),
                (stiffness_hbm, stiffness_ref),
            )
        )
    ]
    for load in small + loads:
        load.start()
    send_u[...] = jnp.zeros_like(send_u)
    send_f[...] = jnp.zeros_like(send_f)

    neighbours = [
        (ix > 0, {"gx": lax.rem(ix + n_x - 1, n_x)}),
        (ix < n_x - 1, {"gx": lax.rem(ix + 1, n_x)}),
        (iy > 0, {"gy": lax.rem(iy + n_y - 1, n_y)}),
        (iy < n_y - 1, {"gy": lax.rem(iy + 1, n_y)}),
    ]

    vectors[...] = jnp.zeros_like(vectors)
    for load in small:
        load.wait()
    for place, ref in enumerate((coords_ref, velocity_ref, external_ref)):
        for j in range(blocks):
            width = min(LANES, modes - j * LANES)
            vectors[place, j : j + 1, :width] = ref[:, j * LANES : j * LANES + width]

    lane = lax.broadcasted_iota(jnp.int32, (LANES, LANES), 1)
    sublane = lax.broadcasted_iota(jnp.int32, (LANES, LANES), 0)
    eye = lane == sublane

    def spread_coords():
        for j in range(blocks):
            height = min(LANES, modes - j * LANES)
            row = jnp.broadcast_to(vectors[0, j : j + 1, :], (height, LANES))
            picked = jnp.where(eye[:height], row, 0.0)
            column[j * LANES : j * LANES + height, :] = jnp.broadcast_to(
                jnp.sum(picked, axis=1, keepdims=True), (height, LANES)
            )

    def fold(product):
        parts = [product[SUB * i : SUB * (i + 1)] for i in range(modes // SUB)]
        while len(parts) > 1:
            nxt = [parts[i] + parts[i + 1] for i in range(0, len(parts) - 1, 2)]
            if len(parts) % 2:
                nxt.append(parts[-1])
            parts = nxt
        return jnp.sum(parts[0], axis=0, keepdims=True)

    def move_tile(t, c):
        rows = raw[c, pl.ds(t, modes, stride=tiles), :]
        phi[c, t] = rows
        table[c, pl.ds(t, 1), :] = fold(rows * column[:modes, :])

    group = 2 if tiles % 2 == 0 else 1

    def displace(g):
        acc = {}
        for i in range(modes // SUB):
            rows = slice(SUB * i, SUB * (i + 1))
            spread = column[rows, :]
            for c in range(3):
                for t in range(group):
                    term = phi[c, g * group + t, rows, :] * spread
                    key = (c, t, i % 2)
                    acc[key] = acc[key] + term if key in acc else term
        for c in range(3):
            for t in range(group):
                table[c, pl.ds(g * group + t, 1), :] = jnp.sum(
                    acc[c, t, 0] + acc[c, t, 1], axis=0, keepdims=True
                )

    low_rows = lax.broadcasted_iota(jnp.int32, (wide, LANES), 0)

    def one_hot(target, chunk, index):
        low = jnp.broadcast_to(index & (wide - 1), (wide, LANES))
        target[:, chunk * LANES : (chunk + 1) * LANES] = jnp.where(
            low == low_rows, 1.0, 0.0
        ).astype(jnp.bfloat16)

    def prepare():
        for chunk in range(corners * chunks):
            one_hot(right_hand, chunk, links_ref[chunk : chunk + 1, :])
        for side in range(4):
            one_hot(right_back, side, senders_ref[side : side + 1, :])

    factor[...] = modulus_ref[...] * weight_ref[...]
    spread_coords()

    for c in range(3):
        loads[c].wait()
        pl.loop(0, tiles)(functools.partial(move_tile, c=c))

    pl.semaphore_wait(barrier, n_x + n_y - 2)

    high_rows = lax.broadcasted_iota(jnp.int32, (groups, LANES), 0)
    contract = (((1,), (1,)), ((), ()))

    def exchange(step, source, target, send_sem, recv_sem):
        copies = []
        for side, (exists, where) in enumerate(neighbours):
            copies.append(
                pltpu.make_async_remote_copy(
                    src_ref=source.at[step, side],
                    dst_ref=target.at[step, side ^ 1],
                    send_sem=send_sem.at[step, side],
                    recv_sem=recv_sem.at[step, side ^ 1],
                    device_id=where,
                    device_id_type=MESH,
                )
            )
        for side, (exists, where) in enumerate(neighbours):
            pl.when(exists)(copies[side].start)
        return copies

    def arrive(step, source, target, send_sem, recv_sem):
        for side, (exists, where) in enumerate(neighbours):
            arrived = pltpu.make_async_remote_copy(
                src_ref=source.at[step, side],
                dst_ref=target.at[step, side],
                send_sem=send_sem.at[step, side],
                recv_sem=recv_sem.at[step, side],
                device_id=where,
                device_id_type=MESH,
            )
            pl.when(exists)(arrived.wait_recv)

    def sent(copies):
        for side, (exists, where) in enumerate(neighbours):
            pl.when(exists)(copies[side].wait_send)

    def total(step, slots, axis, me, size, send_sem, recv_sem):
        copies = []
        for d in range(1, size):
            copies.append(
                pltpu.make_async_remote_copy(
                    src_ref=slots.at[step, me],
                    dst_ref=slots.at[step, me],
                    send_sem=send_sem.at[step, d],
                    recv_sem=recv_sem.at[step, me],
                    device_id={axis: lax.rem(me + d, size)},
                    device_id_type=MESH,
                )
            )
            copies[-1].start()
        for d in range(1, size):
            other = lax.rem(me + d, size)
            pltpu.make_async_remote_copy(
                src_ref=slots.at[step, other],
                dst_ref=slots.at[step, other],
                send_sem=send_sem.at[step, d],
                recv_sem=recv_sem.at[step, other],
                device_id={axis: other},
                device_id_type=MESH,
            ).wait_recv()
        value = slots[step, 0]
        for i in range(1, size):
            value = value + slots[step, i]
        return value, lambda: [copy.wait_send() for copy in copies]

    def gather(index, rows, found):
        low = index & (LANES - 1)
        high = lax.shift_right_logical(index, 7)
        for r, row_of in rows:
            here = high == r
            for c in range(3):
                row = jnp.broadcast_to(row_of(c), index.shape)
                taken = jnp.take_along_axis(row, low, axis=1, mode="promise_in_bounds")
                found[c] = jnp.where(here, taken, found[c])
        return found

    own_rows = [(r, lambda c, r=r: table[c, r : r + 1, :]) for r in range(tiles)]
    senders = jnp.concatenate([senders_ref[...], jnp.zeros((4, LANES), jnp.int32)], axis=0)
    zero = jnp.zeros((chunks, LANES), jnp.float32)

    def place(target, chunk, index, values):
        here = jnp.broadcast_to(lax.shift_right_logical(index, 8), high_rows.shape) == high_rows
        for c, pair in enumerate(values):
            both = [jnp.where(here, jnp.broadcast_to(x, high_rows.shape), 0.0) for x in pair]
            target[2 * c * groups : 2 * (c + 1) * groups, chunk * LANES : (chunk + 1) * LANES] = (
                jnp.concatenate(both, axis=0).astype(jnp.bfloat16)
            )

    def scattered(left, right):
        product = lax.dot_general(
            left[...], right[...], contract, preferred_element_type=jnp.float32
        )
        return [
            product[2 * c * groups : (2 * c + 1) * groups]
            + product[(2 * c + 1) * groups : (2 * c + 2) * groups]
            for c in range(3)
        ]

    def advance(step):
        for c, found in enumerate(
            gather(senders, own_rows, [jnp.zeros((SUB, LANES), jnp.float32)] * 3)
        ):
            for side in range(4):
                send_u[step, side, c : c + 1, :] = found[side : side + 1, :]
        sent_u = exchange(step, send_u, recv_u, u_send_sem, u_recv_sem)
        pl.when(step == 0)(prepare)
        for q in range(corners):
            index = links_ref[q * chunks : (q + 1) * chunks, :]
            for c, found in enumerate(gather(index, own_rows, [zero] * 3)):
                moved[c * corners + q] = found
        arrive(step, send_u, recv_u, u_send_sem, u_recv_sem)
        edge_rows = [
            (tiles + side, lambda c, side=side: recv_u[step, side, c : c + 1, :])
            for side in range(4)
        ]
        corner = [None] * (3 * corners)
        for q in range(corners):
            index = links_ref[q * chunks : (q + 1) * chunks, :]
            begun = [moved[c * corners + q] for c in range(3)]
            for c, found in enumerate(gather(index, edge_rows, begun)):
                corner[c * corners + q] = found
        for i in range(3 * corners):
            strain = stiffness_ref[i, 0] * corner[0]
            for j in range(1, 3 * corners):
                strain = strain + stiffness_ref[i, j] * corner[j]
            force = factor[...] * (strain + strain * strain * strain * (1.0 / 3.0))
            forces[0, i], forces[1, i] = split(force)
        for q in range(corners):
            for s in range(chunks):
                chunk = q * chunks + s
                place(
                    left_hand,
                    chunk,
                    links_ref[chunk : chunk + 1, :],
                    [
                        [forces[h, c * corners + q, s : s + 1, :] for h in range(2)]
                        for c in range(3)
                    ],
                )
        for c, both in enumerate(scattered(left_hand, right_hand)):
            for half in range(2):
                own_force[c, half] = both[:, half * LANES : (half + 1) * LANES]
            for side in range(4):
                row, half = (tiles + side) // 2, (tiles + side) % 2
                send_f[step, side, c : c + 1, :] = both[
                    row : row + 1, half * LANES : (half + 1) * LANES
                ]
        sent_f = exchange(step, send_f, recv_f, f_send_sem, f_recv_sem)
        arrive(step, send_f, recv_f, f_send_sem, f_recv_sem)
        for side in range(4):
            place(
                left_back,
                side,
                senders_ref[side : side + 1, :],
                [split(recv_f[step, side, c : c + 1, :]) for c in range(3)],
            )
        for c, both in enumerate(scattered(left_back, right_back)):
            for half in range(2):
                own_force[c, half] += both[:, half * LANES : (half + 1) * LANES]

        height = 10 * SUB if modes % (10 * SUB) == 0 else SUB

        @pl.loop(0, modes // height)
        def _(b):
            rows = pl.ds(pl.multiple_of(b * height, SUB), height)
            acc = [None] * 3
            for c in range(3):
                for t in range(tiles):
                    term = phi[c, t, rows, :] * jnp.broadcast_to(
                        own_force[c, t % 2, t // 2 : t // 2 + 1, :], (height, LANES)
                    )
                    acc[c] = term if acc[c] is None else acc[c] + term
            column[rows, :] = jnp.broadcast_to(
                jnp.sum(acc[0] + acc[1] + acc[2], axis=1, keepdims=True), (height, LANES)
            )

        for j in range(blocks):
            rows = min(LANES, modes - j * LANES)
            picked = jnp.where(eye[:rows], column[j * LANES : j * LANES + rows, :], 0.0)
            sum_x[step, ix, j : j + 1, :] = jnp.sum(picked, axis=0, keepdims=True)
        along_x, sent_x = total(step, sum_x, "gx", ix, n_x, x_send_sem, x_recv_sem)
        sum_y[step, iy] = along_x
        reduced, sent_y = total(step, sum_y, "gy", iy, n_y, y_send_sem, y_recv_sem)
        velocity = vectors[1] + time_step * (vectors[2] - reduced)
        vectors[3] = reduced
        vectors[1] = velocity
        vectors[0] = vectors[0] + time_step * velocity
        spread_coords()
        pl.loop(0, tiles // group)(displace)
        sent(sent_u)
        sent(sent_f)
        sent_x()
        sent_y()

    pl.loop(0, STEPS)(advance)

    for place_out, slot in enumerate((0, 1, 3)):
        packed_out[place_out * blocks : (place_out + 1) * blocks, :] = vectors[slot]
    for c in range(3):
        first = 3 * blocks + c * tiles
        packed_out[first : first + tiles, :] = table[c, :tiles, :]


def unpack(packed, coords_out, velocity_out, reduced_out, displaced_out):
    modes = coords_out.shape[1]
    blocks = pl.cdiv(modes, LANES)
    for slot, ref in enumerate((coords_out, velocity_out, reduced_out)):
        for j in range(blocks):
            width = min(LANES, modes - j * LANES)
            row = slot * blocks + j
            ref[:, j * LANES : j * LANES + width] = packed[row : row + 1, :width]
    tiles = displaced_out.shape[2] // LANES
    for c in range(3):
        for t in range(tiles):
            row = 3 * blocks + c * tiles + t
            displaced_out[c, :, t * LANES : (t + 1) * LANES] = packed[row : row + 1, :]


def shards(
    basis, connectivity, send_nodes, modulus, ecsw_weight, stiffness, coords, velocity, external
):
    modes, nodes = basis.shape[1], basis.shape[3]
    corners, elements = connectivity.shape[0], connectivity.shape[2]
    tiles, chunks = nodes // LANES, elements // LANES
    n_x, n_y = lax.axis_size("gx"), lax.axis_size("gy")
    blocks = pl.cdiv(modes, LANES)
    groups = pl.cdiv(pl.cdiv(tiles + 4, 2), SUB) * SUB
    wide = 2 * LANES
    f32 = jnp.float32
    vmem = pl.BlockSpec(memory_space=pltpu.VMEM)
    tile = (4, LANES)
    dma = pltpu.SemaphoreType.DMA
    packed = pl.pallas_call(
        functools.partial(kernel, (modes, tiles, corners, chunks, n_x, n_y)),
        out_shape=jax.ShapeDtypeStruct((3 * blocks + 3 * tiles, LANES), f32),
        in_specs=[pl.BlockSpec(memory_space=pl.ANY)] * 9,
        out_specs=vmem,
        scratch_shapes=[
            pltpu.VMEM((corners * chunks, LANES), jnp.int32),
            pltpu.VMEM((4, LANES), jnp.int32),
            pltpu.VMEM((chunks, LANES), f32),
            pltpu.VMEM((chunks, LANES), f32),
            pltpu.SMEM(stiffness.shape, f32),
            pltpu.VMEM((1, modes), f32),
            pltpu.VMEM((1, modes), f32),
            pltpu.VMEM((1, modes), f32),
            dma((8,)),
            pltpu.VMEM((3, modes * tiles, LANES), f32),
            pltpu.VMEM((3, tiles, modes, LANES), f32),
            pltpu.VMEM((blocks * LANES, LANES), f32),
            pltpu.VMEM((4, blocks, LANES), f32),
            pltpu.VMEM((3, tiles, LANES), f32),
            pltpu.VMEM((chunks, LANES), f32),
            pltpu.VMEM((3 * corners, chunks, LANES), f32),
            pltpu.VMEM((2, 3 * corners, chunks, LANES), f32),
            pltpu.VMEM((6 * groups, corners * elements), jnp.bfloat16),
            pltpu.VMEM((wide, corners * elements), jnp.bfloat16),
            pltpu.VMEM((6 * groups, 4 * LANES), jnp.bfloat16),
            pltpu.VMEM((wide, 4 * LANES), jnp.bfloat16),
            pltpu.VMEM((3, 2, groups, LANES), f32),
            pltpu.VMEM((STEPS, 4) + tile, f32),
            pltpu.VMEM((STEPS, 4) + tile, f32),
            pltpu.VMEM((STEPS, 4) + tile, f32),
            pltpu.VMEM((STEPS, 4) + tile, f32),
            pltpu.VMEM((STEPS, n_x, blocks, LANES), f32),
            pltpu.VMEM((STEPS, n_y, blocks, LANES), f32),
            dma((3,)),
            dma((STEPS, 4)),
            dma((STEPS, 4)),
            dma((STEPS, 4)),
            dma((STEPS, 4)),
            dma((STEPS, n_x)),
            dma((STEPS, n_x)),
            dma((STEPS, n_y)),
            dma((STEPS, n_y)),
        ],
        compiler_params=pltpu.CompilerParams(collective_id=0, has_side_effects=True),
    )(
        basis.reshape(3 * modes * tiles, LANES),
        connectivity.reshape(corners * chunks, LANES),
        send_nodes.reshape(4, LANES),
        modulus.reshape(chunks, LANES),
        ecsw_weight.reshape(chunks, LANES),
        stiffness,
        coords.reshape(1, modes),
        velocity.reshape(1, modes),
        external.reshape(1, modes),
    )
    coords, velocity, reduced, displaced = pl.pallas_call(
        unpack,
        out_shape=[jax.ShapeDtypeStruct((1, modes), f32)] * 3
        + [jax.ShapeDtypeStruct((3, 1, nodes), f32)],
        in_specs=[vmem],
        out_specs=[vmem] * 4,
    )(packed)
    return (
        coords.reshape(modes),
        velocity.reshape(modes),
        reduced.reshape(modes),
        displaced,
    )


def solution(mesh):
    return jax.shard_map(
        shards,
        mesh=mesh,
        in_specs=(
            P(None, None, "gx", "gy"),
            P(None, "gx", "gy"),
            P(None, "gx", "gy"),
            P("gx", "gy"),
            P("gx", "gy"),
            P(),
            P(),
            P(),
            P(),
        ),
        out_specs=(P(), P(), P(), P(None, "gx", "gy")),
        check_vma=False,
    )
```
